256 devices in a mesh: tm: 64 (over z, x, core), row: 4 (over y).
Axes of the slice: x: 4, y: 4, z: 8, core: 2. Of those that a mesh axis runs over, the one named last changes fastest.
Arguments:
- filter_map: bfloat16 [1024, 256, 256], P('tm', 'row'), may hold values from -1 to 1
- filter_cov: bfloat16 [1024, 256, 256], P('tm', 'row'), may hold values from -1 to 1
- smoother_gain: bfloat16 [1024, 256, 256], P('tm', 'row'), may hold values from -1 to 1
- transition: bfloat16 [256, 256], replicated, may hold values from -0.375 to 0.375
- site_basis: bfloat16 [2048, 256], replicated, may hold values from -0.375 to 0.375
- obs_time: int32 [32768], P('tm'), may hold values from 0 to 1023, as said below
- obs_site: int32 [32768], P('tm'), may hold values from 0 to 2047
- obs_value: float32 [32768, 128], P('tm'), may hold values from -6 to 6
- obs_weight: float32 [32768], P('tm'), may hold values from 0.5 to 8
Outputs:
- smoothed: float32 [1024, 256, 128], P('tm', 'row')
The draws below stay inside these ranges and needn't reach their ends.
Inputs may be any that keep to these rules, and one draw needn't show every extreme that they name: `obs_time`: row r has a time step from (r // 512) * 16 to (r // 512 + 1) * 16 - 1; rows are in no order of time.
All inputs are finite; a program needn't handle non-finite values.
Results may differ from the reference program's by a relative error of at most 0.0041.
Values may be sent and summed in bfloat16 or wider, within the bound.
No kernel may reach another device: no remote copies, remote signals or barrier semaphores. Data moves between devices by JAX's collectives and lax.ppermute only.
A program may use at most 128 MiB of HBM per device.

```python
import math
import jax
import jax.numpy as jnp
from jax import lax

D = 256
SITES = 2048
ENS = 128
STEPS_DEV = 16
OBS_DEV = 512
TIME_STEP_TOTAL = 1024
OBS = 32768
N_TM = 64


def bit_parity(first_index, second_index, limit):
    count = first_index * second_index * 0
    place = 1
    while place < limit:
        first_bit = first_index // place % 2
        second_bit = second_index // place % 2
        count = count + first_bit * second_bit
        place = place * 2
    return count % 2


def dynamics(key):
    shuffled = jax.random.permutation(jax.random.fold_in(key, 11), D)
    slot_index = jnp.argsort(shuffled).astype(jnp.int32)
    half_width = D // 2
    quarter = D // 4
    channel_group = slot_index // half_width
    within = slot_index % half_width
    side_index = within // quarter
    sub_index = within % quarter
    same_group = (channel_group[:, None] == channel_group[None, :]).astype(jnp.float32)
    parity = bit_parity(sub_index[:, None], sub_index[None, :], quarter)
    hadamard = (1.0 - 2.0 * parity.astype(jnp.float32)) / quarter ** 0.5
    turning = (side_index[None, :] - side_index[:, None]).astype(jnp.float32)
    sign_flips = jnp.where(jax.random.bernoulli(jax.random.fold_in(key, 12), 0.5, (TIME_STEP_TOTAL, D)), 1.0, -1.0)
    skew_part = sign_flips[:, :, None] * sign_flips[:, None, :] * (hadamard * turning)[None]
    rotation = same_group[None] * (0.8 * jnp.eye(D, dtype=jnp.float32)[None] + 0.6 * skew_part)
    rate_key = jax.random.fold_in(key, 13)
    slow_rate = jnp.exp(jax.random.uniform(rate_key, (D,), minval=jnp.log(0.05), maxval=jnp.log(0.5))) / TIME_STEP_TOTAL
    fast_rate = jnp.exp(jax.random.uniform(jax.random.fold_in(key, 15), (D,), minval=jnp.log(0.05), maxval=jnp.log(0.1)))
    falloff_speed = jnp.where(channel_group == 0, slow_rate, fast_rate)
    leakage = jax.random.normal(jax.random.fold_in(key, 14), (TIME_STEP_TOTAL, D, D))
    factor = jnp.exp(jax.random.uniform(jax.random.fold_in(key, 16), (N_TM,), minval=jnp.log(0.5), maxval=jnp.log(2.0)))
    per_step_multiplier = jnp.repeat(factor, STEPS_DEV)
    spike_position = jax.random.randint(jax.random.fold_in(key, 17), (3,), 0, TIME_STEP_TOTAL)
    forcing_magnitude = jax.random.uniform(jax.random.fold_in(key, 18), (3,), minval=0.5, maxval=0.8)
    time_step_index = jnp.arange(TIME_STEP_TOTAL, dtype=jnp.int32)
    spike_scale = jnp.prod(jnp.where(time_step_index[:, None] == spike_position[None, :], forcing_magnitude[None, :], 1.0), axis=1)
    retained_fraction = jnp.exp(-falloff_speed[None, :] * per_step_multiplier[:, None]) * spike_scale[:, None]
    matrix = retained_fraction[:, :, None] * (rotation + 0.02 * leakage / D ** 0.5)
    return matrix


def draw_filter_map(key, part):
    return dynamics(jax.random.fold_in(key, 1)).astype(jnp.bfloat16)


def draw_smoother_gain(key, part):
    return dynamics(jax.random.fold_in(key, 2)).astype(jnp.bfloat16)


def draw_filter_cov(key, part):
    noise_key = jax.random.fold_in(key, 3)
    diagonal_key = jax.random.fold_in(key, 4)
    noise_part = jax.random.normal(noise_key, (TIME_STEP_TOTAL, D, D))
    diagonal = jnp.exp(jax.random.uniform(diagonal_key, (TIME_STEP_TOTAL, D), minval=jnp.log(0.5), maxval=jnp.log(2.0)))
    symmetric = (noise_part + jnp.swapaxes(noise_part, 1, 2)) * (0.4 / (2 * D) ** 0.5)
    matrix = diagonal[:, :, None] * jnp.eye(D, dtype=jnp.float32)[None] + symmetric
    return (matrix / TIME_STEP_TOTAL).astype(jnp.bfloat16)


def draw_obs_time(key, part):
    block_index = jnp.arange(OBS_DEV * N_TM, dtype=jnp.int32) // OBS_DEV
    offset = jax.random.randint(jax.random.fold_in(key, 5), (OBS_DEV * N_TM,), 0, STEPS_DEV)
    return (block_index * STEPS_DEV + offset).astype(jnp.int32)


def plant(array, own_key, least, top_value):
    shape = array.shape
    index_at = [jax.random.randint(jax.random.fold_in(own_key, axis), (), 0, shape[axis]) for axis in range(len(shape))]
    array = array.at[tuple(index_at)].set(least)
    longest = shape.index(max(shape))
    index_at[longest] = (index_at[longest] + 1) % shape[longest]
    return array.at[tuple(index_at)].set(top_value)


def levels(stream_key, dims, pieces, least, high):
    loudness, own = 1.0, jax.random.fold_in(stream_key, 6)
    for axis_at, parts in pieces:
        steps = jnp.exp(jax.random.uniform(jax.random.fold_in(own, axis_at), (parts,), jnp.float32, least / len(pieces), high / len(pieces)))
        loudness = loudness * jnp.repeat(steps, dims[axis_at] // parts).reshape([-1 if axis == axis_at else 1 for axis in range(len(dims))])
    return loudness


def centred(stream_key, shape, spread, reach, split=(), held_as=jnp.bfloat16):
    drawn = spread * jax.random.normal(stream_key, shape, jnp.float32)
    if split:
        drawn = drawn * levels(stream_key, shape, split, -0.22, 0.18)
    return jnp.clip(drawn, -reach, reach).astype(held_as)


def setup_inputs(seed: int = 0) -> dict:
    keys = jax.random.split(jax.random.key(seed), 10)
    return {
        "filter_map": draw_filter_map(jax.random.fold_in(keys[9], 71), 0),
        "filter_cov": draw_filter_cov(jax.random.fold_in(keys[9], 71), 0),
        "smoother_gain": draw_smoother_gain(jax.random.fold_in(keys[9], 71), 0),
        "transition": centred(keys[3], (D, D), D ** -0.5, 0.375),
        "site_basis": centred(keys[4], (SITES, D), D ** -0.5, 0.375),
        "obs_time": draw_obs_time(jax.random.fold_in(keys[9], 71), 0),
        "obs_site": plant(jax.random.randint(keys[6], (OBS,), 0, SITES), jax.random.fold_in(keys[6], 1), 0, SITES - 1).astype(jnp.int32),
        "obs_value": centred(keys[7], (OBS, ENS), 1.0, 6.0, ((0, 64),), jnp.float32),
        "obs_weight": jnp.clip(jnp.exp(math.log(8.0) - 2.7725887 * jax.random.uniform(keys[8], (OBS,), jnp.float32) ** levels(keys[8], (OBS,), ((0, 64),), -0.2, 0.2)), 0.5, 8.0),
    }


highest = lax.Precision.HIGHEST


def product(first_factor, second_factor):
    return jnp.dot(first_factor, second_factor, precision=highest, preferred_element_type=jnp.float32)


def reference(filter_map, filter_cov, smoother_gain, transition, site_basis, obs_time, obs_site, obs_value, obs_weight):
    weighted = (obs_weight[:, None] * obs_value).astype(jnp.bfloat16)
    weighted = lax.optimization_barrier(weighted).astype(jnp.float32)
    basis_rows = jnp.take(site_basis, obs_site, axis=0).astype(jnp.float32)
    block_basis = basis_rows.reshape(N_TM, OBS_DEV, D)
    block_weighted = weighted.reshape(N_TM, OBS_DEV, ENS)
    block_times = obs_time.reshape(N_TM, OBS_DEV)

    def block_info(inputs):
        block_index, basis_part, weighted_part, times_part = inputs
        local_step = (times_part - block_index * STEPS_DEV).astype(jnp.int32)
        outer_terms = basis_part[:, :, None] * weighted_part[:, None, :]
        return jax.ops.segment_sum(outer_terms, local_step, num_segments=STEPS_DEV)

    information = lax.map(block_info, (jnp.arange(N_TM, dtype=jnp.int32), block_basis, block_weighted, block_times))
    information = information.reshape(TIME_STEP_TOTAL, D, ENS).astype(jnp.bfloat16)

    def forward(current, inputs):
        matrix, covariance, information_step = inputs
        drive_step = jnp.dot(covariance, information_step, preferred_element_type=jnp.float32)
        current = product(matrix.astype(jnp.float32), current) + drive_step
        return current, current

    anchor = jnp.zeros((D, ENS), jnp.float32)
    filtered = lax.scan(forward, anchor, (filter_map, filter_cov, information))[1]
    transition_wide = transition.astype(jnp.float32)

    def backward(current, inputs):
        gain_matrix, filtered_mean = inputs
        gain_wide = gain_matrix.astype(jnp.float32)
        offset = filtered_mean - product(gain_wide, product(transition_wide, filtered_mean))
        current = product(gain_wide, current) + offset
        return current, current

    earlier = lax.scan(backward, filtered[-1], (smoother_gain[:-1], filtered[:-1]), reverse=True)[1]
    return jnp.concatenate([earlier, filtered[-1:]], axis=0)
```

```python
import jax
import jax.numpy as jnp
from jax import lax
from jax.experimental import pallas as pl
from jax.experimental.pallas import tpu as pltpu
from jax.sharding import Mesh, PartitionSpec as P

BF = jnp.bfloat16
F32 = jnp.float32
NZ, NX, NC, NR = 8, 4, 2, 4
NT = (((1,), (1,)), ((), ()))
VM = pl.BlockSpec(memory_space=pltpu.VMEM)
HB = pl.BlockSpec(memory_space=pltpu.HBM)
SM = pl.BlockSpec(memory_space=pltpu.SMEM)


def split(value):
    hi = value.astype(BF)
    return hi, (value - hi.astype(F32)).astype(BF)


def mm(left, right):
    return jnp.dot(left, right, preferred_element_type=F32)


def mm3(left_hi, left_lo, right_hi, right_lo):
    return mm(left_hi, right_hi) + (mm(left_hi, right_lo) + mm(left_lo, right_hi))


def push(state, weight):
    hi, lo = split(state)
    both = lax.dot_general(
        jnp.concatenate([hi, lo], axis=0), weight, NT, preferred_element_type=F32
    )
    n = state.shape[0]
    return both[:n] + both[n:]


def push2(state, weight_hi, weight_lo):
    hi, lo = split(state)
    both = lax.dot_general(
        jnp.concatenate([hi, lo], axis=0), weight_hi, NT, preferred_element_type=F32
    )
    n = state.shape[0]
    extra = lax.dot_general(hi, weight_lo, NT, preferred_element_type=F32)
    return both[:n] + (both[n:] + extra)


def coords(idx_ref):
    me = idx_ref[0]
    row = me % NR
    tm = me // NR
    return tm // (NX * NC), (tm // NC) % NX, tm % NC, row


def call(body, outs, *args, scratch=(), far_in=(), far_out=()):
    many = isinstance(outs, tuple)
    count = len(outs) if many else 1
    specs = tuple(HB if i in far_out else VM for i in range(count))
    far = len(far_in) + len(far_out)
    if many:
        outs = tuple(
            pltpu.HBM(o.shape, o.dtype) if i in far_out else o for i, o in enumerate(outs)
        )
    args = [args[0]] + [
        pltpu.with_memory_space_constraint(a, pltpu.HBM) if i in far_in else a
        for i, a in enumerate(args[1:])
    ]
    return pl.pallas_call(
        body,
        out_shape=outs,
        in_specs=[SM] + [HB if i in far_in else VM for i in range(len(args) - 1)],
        out_specs=specs if many else specs[0],
        scratch_shapes=list(scratch) + ([pltpu.SemaphoreType.DMA((far,))] if far else []),
        compiler_params=pltpu.CompilerParams(vmem_limit_bytes=16 << 20),
    )(*args)


def shape(dims, dtype):
    return jax.ShapeDtypeStruct(dims, dtype)


def drive_body(idx, basis, value, weight, time, cov, *outs):
    row = idx[0] % NR
    steps = cov.shape[0]
    weighted = (weight[...] * jnp.transpose(value[...])).astype(BF)
    local_time = time[...] - (idx[0] // NR) * steps
    half = steps // 2
    members = weighted.shape[0] // NR
    for k in range(steps):
        masked = jnp.where(local_time == k, weighted, jnp.zeros((), BF))
        info = mm(masked, basis[...]).astype(BF)
        drive = lax.dot_general(info, cov[k], NT, preferred_element_type=F32)
        w = drive.shape[1]
        lane = (k // half) * w
        for s, out in enumerate(outs):
            part = drive[0:members]
            for r in range(1, NR):
                part = jnp.where((row + s) % NR == r, drive[r * members : (r + 1) * members], part)
            out[k % half, :, lane : lane + w] = part


def assemble(row, parts, full):
    w = parts[0].shape[1]
    for s, part in enumerate(parts):
        start = pl.multiple_of(((row - s) % NR) * w, w)
        full[:, pl.ds(start, w), :] = part[...]


def tree(items, order):
    while len(items) > 1:
        merged = []
        for i in range(0, len(items), 2):
            left, right = order(items[i], items[i + 1])
            if left[1] is None:
                value = mm(left[0], right[0])
            else:
                value = mm3(left[0], left[1], right[0], right[1])
            merged.append(split(value))
        items = merged
    return items[0]


def later_first(a, b):
    return b, a


def earlier_first(a, b):
    return a, b


def fwd_local_body(idx, m0, m1, m2, m3, full, packed):
    _, _, _, row = coords(idx)
    assemble(row, (m0, m1, m2, m3), full)
    steps, n = full.shape[0], full.shape[1]
    hi, lo = tree([(full[k], None) for k in range(steps)], later_first)
    packed[0:n] = hi
    packed[n:] = lo


def fwd_drive_body(idx, full, d0, d1, d2, d3, far_full, far_drives, msg, drv, drives, sems):
    _, _, _, row = coords(idx)
    save_full = pltpu.make_async_copy(full, far_full, sems.at[0])
    save_full.start()
    for s, part in enumerate((d0, d1, d2, d3)):
        drv[(row - s) % NR] = part[...]
    steps, n = full.shape[0], full.shape[1]
    half, w = steps // 2, n // NR
    for k in range(steps):
        lane = (k // half) * w
        drives[k] = jnp.concatenate(
            [drv[r, k % half, :, lane : lane + w] for r in range(NR)], axis=1
        )
    save_drives = pltpu.make_async_copy(drives, far_drives, sems.at[1])
    save_drives.start()
    b = drives[0]
    for k in range(1, steps):
        b = push(b, full[k]) + drives[k]
    store_pair(msg, b)
    save_full.wait()
    save_drives.wait()


def store_pair(msg, b):
    m = b.shape[0]
    hi, lo = split(b)
    msg[0:m] = hi
    msg[m:] = lo


def load_pair(msg):
    m = msg.shape[0] // 2
    return msg[0:m].astype(F32) + msg[m:].astype(F32)


def fwd_core_body(idx, own, other, b_own, b_other, far_other, far_b, keep, msg, sems):
    save_other = pltpu.make_async_copy(other, far_other, sems.at[0])
    save_b = pltpu.make_async_copy(b_other, far_b, sems.at[1])
    save_other.start()
    save_b.start()
    _, _, c, _ = coords(idx)
    n = own.shape[1]
    m = b_own.shape[0] // 2
    first = jnp.where(c == 0, own[...], other[...])
    second = jnp.where(c == 0, other[...], own[...])
    hi, lo = split(mm3(second[0:n], second[n:], first[0:n], first[n:]))
    b_mine, b_theirs = load_pair(b_own), load_pair(b_other)
    b_first = jnp.where(c == 0, b_mine, b_theirs)
    b_second = jnp.where(c == 0, b_theirs, b_mine)
    b = push2(b_first, second[0:n], second[n:]) + b_second
    w = n // NC
    keep[0:n] = hi
    keep[n : 2 * n] = lo
    b_hi, b_lo = split(b)
    keep[2 * n : 2 * n + m] = b_hi
    keep[2 * n + m :] = b_lo
    msg[0:n] = half_of(c, hi, w)
    msg[n : 2 * n] = half_of(c, lo, w)
    msg[2 * n :] = pack_vector(c, b)
    save_other.wait()
    save_b.wait()


def half_of(c, value, w):
    return jnp.where(c == 0, value[:, :w], value[:, w:])


def pack_vector(c, b):
    m, n = b.shape
    w, q = n // NC, m // NC
    hi, lo = split(jnp.where(c == 0, b[:q], b[q:]))
    return jnp.concatenate([hi[:, :w], hi[:, w:], lo[:, :w], lo[:, w:]], axis=0)


def unpack_part(msg, at, q):
    p = [msg[at + j * q : at + (j + 1) * q].astype(F32) for j in range(4)]
    return jnp.concatenate([p[0] + p[2], p[1] + p[3]], axis=1)


def unpack_vector(c, mine, other, at, m):
    q = m // NC
    a, b = unpack_part(mine, at, q), unpack_part(other, at, q)
    return jnp.concatenate([jnp.where(c == 0, a, b), jnp.where(c == 0, b, a)], axis=0)


def join(c, mine, other, rows):
    a, b = mine[0:rows], other[0:rows]
    return jnp.concatenate([jnp.where(c == 0, a, b), jnp.where(c == 0, b, a)], axis=1)


def fwd_x_body(idx, own, r1, r2, r3, s1, s2, s3, far_ax, far_bx, msg, ax, bx, sems):
    _, x, c, _ = coords(idx)
    rows, n = ax.shape[1:]
    m = bx.shape[1]
    for s, (mine, other) in enumerate(((own, None), (r1, s1), (r2, s2), (r3, s3))):
        at = (x - s) % NX
        if other is None:
            ax[at] = mine[0:rows]
            bx[at] = mine[rows : rows + m].astype(F32) + mine[rows + m :].astype(F32)
        else:
            ax[at] = join(c, mine, other, rows)
            bx[at] = unpack_vector(c, mine, other, rows, m)
    save_ax = pltpu.make_async_copy(ax, far_ax, sems.at[0])
    save_bx = pltpu.make_async_copy(bx, far_bx, sems.at[1])
    save_ax.start()
    save_bx.start()
    hi, _ = tree([(ax[i, 0:n], ax[i, n:]) for i in range(NX)], later_first)
    b = bx[0]
    for i in range(1, NX):
        b = push2(b, ax[i, 0:n], ax[i, n:]) + bx[i]
    hi = half_of(c, hi, n // NC)
    packed = pack_vector(c, b)
    for i in range(NZ):
        msg[i, 0:n] = hi
        msg[i, n:] = packed
    save_ax.wait()
    save_bx.wait()


def bwd_local_body(idx, g0, g1, g2, g3, far_full, packed, full, sems):
    _, _, _, row = coords(idx)
    assemble(row, (g0, g1, g2, g3), full)
    steps, n = full.shape[0], full.shape[1]

    @pl.when(idx[0] // NR == NZ * NX * NC - 1)
    def _():
        full[steps - 1] = jnp.zeros((n, n), BF)

    save_full = pltpu.make_async_copy(full, far_full, sems.at[0])
    save_full.start()
    hi, lo = tree([(full[k], None) for k in range(steps)], earlier_first)
    packed[0:n] = hi
    packed[n:] = lo
    save_full.wait()


def bwd_core_body(idx, own, other, out):
    _, _, c, _ = coords(idx)
    n = own.shape[1]
    first = jnp.where(c == 0, own[...], other[...])
    second = jnp.where(c == 0, other[...], own[...])
    hi, lo = split(mm3(first[0:n], first[n:], second[0:n], second[n:]))
    out[0:n] = hi
    out[n:] = lo


def bwd_x_body(idx, m0, m1, m2, m3, far_cx, msg, cx, sems):
    _, x, c, _ = coords(idx)
    n = cx.shape[2]
    for s, part in enumerate((m0, m1, m2, m3)):
        cx[(x - s) % NX] = part[...]
    save_cx = pltpu.make_async_copy(cx, far_cx, sems.at[0])
    save_cx.start()
    hi, _ = tree([(cx[i, 0:n], cx[i, n:]) for i in range(NX)], earlier_first)
    hi = half_of(c, hi, n // NC)
    for i in range(NZ):
        msg[i] = hi
    save_cx.wait()


def load(sems, at, *pairs):
    copies = []
    for i, (far, close) in enumerate(pairs):
        copy = pltpu.make_async_copy(far, close, sems.at[at + i])
        copy.start()
        copies.append(copy)
    return copies


def fetch_body(idx, far, out, sems):
    copy = pltpu.make_async_copy(far, out, sems.at[0])
    copy.start()
    copy.wait()


def filter_body(
    idx, mine, swapped, b_other, far_other, far_transition, far_ax, far_bx, far_full, far_drives, far_gains,
    far_off, msg, other, transition, ax, bx, full, drives, gains, off, sems,
):
    z, x, c, _ = coords(idx)
    steps, n = full.shape[0], full.shape[1]
    m = drives.shape[1]
    get_ax, get_bx, get_other, get_drives, get_full, get_gains, get_transition = load(
        sems, 0, (far_ax, ax), (far_bx, bx), (far_other, other), (far_drives, drives),
        (far_full, full), (far_gains, gains), (far_transition, transition),
    )
    state = jnp.zeros((m, n), F32)
    for i in range(NZ - 1):
        b = unpack_vector(c, mine.at[i], swapped.at[i], n, m)
        moved = push(state, join(c, mine.at[i], swapped.at[i], n)) + b
        state = jnp.where(i < z, moved, state)
    get_ax.wait()
    get_bx.wait()
    for i in range(NX - 1):
        moved = push2(state, ax[i, 0:n], ax[i, n:]) + bx[i]
        state = jnp.where(i < x, moved, state)
    get_other.wait()
    moved = push2(state, other[0:n], other[n:]) + load_pair(b_other)
    state = jnp.where(c == 1, moved, state)
    get_drives.wait()
    get_full.wait()
    for k in range(steps):
        state = push(state, full[k]) + drives[k]
        drives[k] = state
    get_gains.wait()
    get_transition.wait()
    weight = transition[...]
    for k in range(steps):
        mean = drives[k]
        off[k] = mean - push(push(mean, weight), gains[k])
    save_off = pltpu.make_async_copy(off, far_off, sems.at[7])
    save_off.start()
    f = off[steps - 1]
    for k in range(steps - 2, -1, -1):
        f = push(f, gains[k]) + off[k]
    store_pair(msg, f)
    save_off.wait()


def back_core_body(idx, own, other, cown, cother, out):
    _, _, c, _ = coords(idx)
    n = own.shape[1]
    f_own, f_other = load_pair(own), load_pair(other)
    f0 = jnp.where(c == 0, f_own, f_other)
    f1 = jnp.where(c == 0, f_other, f_own)
    hi = jnp.where(c == 0, cown[0:n], cother[0:n])
    lo = jnp.where(c == 0, cown[n:], cother[n:])
    out[...] = push2(f1, hi, lo) + f0


def back_x_body(idx, f0, f1, f2, f3, far_cx, fx, out, cx, sems):
    (get_cx,) = load(sems, 0, (far_cx, cx))
    _, x, _, _ = coords(idx)
    n = fx.shape[2]
    for s, part in enumerate((f0, f1, f2, f3)):
        fx[(x - s) % NX] = part[...]
    get_cx.wait()
    f = fx[NX - 1]
    for i in range(NX - 2, -1, -1):
        f = push2(f, cx[i, 0:n], cx[i, n:]) + fx[i]
    for i in range(NZ):
        out[i] = f


def smooth_body(
    idx, mine, swapped, fz, fx, fother, cother, far_cx, far_gains, far_off, o0, o1, o2, o3,
    cx, gains, off, sems,
):
    get_cx, get_gains, get_off = load(
        sems, 0, (far_cx, cx), (far_gains, gains), (far_off, off)
    )
    z, x, c, row = coords(idx)
    steps, n = gains.shape[0], gains.shape[1]
    m = off.shape[1]
    half, w = steps // 2, n // NR
    state = jnp.zeros((m, n), F32)
    for i in range(NZ - 1, 0, -1):
        moved = push(state, join(c, mine.at[i], swapped.at[i], n)) + fz[i].astype(F32)
        state = jnp.where(i > z, moved, state)
    get_cx.wait()
    for i in range(NX - 1, 0, -1):
        moved = push2(state, cx[i, 0:n], cx[i, n:]) + fx[i]
        state = jnp.where(i > x, moved, state)
    moved = push2(state, cother[0:n], cother[n:]) + load_pair(fother)
    state = jnp.where(c == 0, moved, state)
    get_gains.wait()
    get_off.wait()
    for k in range(steps - 1, -1, -1):
        state = push(state, gains[k]) + off[k]
        lane = (k // half) * w
        parts = [state[:, r * w : (r + 1) * w].astype(BF) for r in range(NR)]
        for s, out in enumerate((o0, o1, o2, o3)):
            part = parts[0]
            for r in range(1, NR):
                part = jnp.where((row + s) % NR == r, parts[r], part)
            out[k % half, :, lane : lane + w] = part


def place_body(idx, p0, p1, p2, p3, out, got):
    _, _, _, row = coords(idx)
    half = out.shape[0] // 2
    w = out.shape[1]
    for s, part in enumerate((p0, p1, p2, p3)):
        got[(row - s) % NR] = part[...]
    for k in range(half):
        block = jnp.concatenate([got[r, k] for r in range(NR)], axis=0).astype(F32)
        turned = jnp.transpose(block)
        out[k] = turned[:w]
        out[k + half] = turned[w:]


def shift(value, axis, step, size):
    return lax.ppermute(value, axis, [(i, (i + step) % size) for i in range(size)])


def spread(value, axis):
    return lax.all_to_all(value, axis, 0, 0, tiled=True)


def swap(value):
    return lax.ppermute(value, "c", [(0, 1), (1, 0)])


def gather_rows(value):
    return [value] + [shift(value, "row", s, NR) for s in range(1, NR)]


def local(
    filter_map,
    filter_cov,
    smoother_gain,
    transition,
    site_basis,
    obs_time,
    obs_site,
    obs_value,
    obs_weight,
):
    steps, w, n = filter_map.shape
    obs, members = obs_value.shape
    m = members // NR
    half = steps // 2
    tm = (lax.axis_index("z") * NX + lax.axis_index("x")) * NC + lax.axis_index("c")
    idx = (tm * NR + lax.axis_index("row")).astype(jnp.int32).reshape(1)

    maps = gather_rows(filter_map)
    basis_rows = site_basis.at[obs_site].get(mode="promise_in_bounds")
    drive = call(
        drive_body,
        (shape((half, m, 2 * w), F32),) * NR,
        idx,
        basis_rows,
        obs_value,
        obs_weight.reshape(1, obs),
        obs_time.reshape(1, obs),
        filter_cov,
    )
    gain_in, _ = lax.optimization_barrier((smoother_gain, drive))
    drive = drive[:1] + tuple(shift(drive[s], "row", s, NR) for s in range(1, NR))
    gains = gather_rows(gain_in)
    full, packed = call(
        fwd_local_body,
        (shape((steps, n, n), BF), shape((2 * n, n), BF)),
        idx,
        *maps,
    )
    packed_other = swap(packed)
    full, drives, bmsg = call(
        fwd_drive_body,
        (shape((steps, n, n), BF), shape((steps, m, n), F32), shape((2 * m, n), BF)),
        idx,
        full,
        *drive,
        scratch=[pltpu.VMEM((NR, half, m, 2 * w), F32), pltpu.VMEM((steps, m, n), F32)],
        far_out=(0, 1),
    )
    bmsg_other = swap(bmsg)
    far_other, far_b, keep, msg = call(
        fwd_core_body,
        (
            shape((2 * n, n), BF),
            shape((2 * m, n), BF),
            shape((2 * n + 2 * m, n), BF),
            shape((2 * n + 2 * m, n // NC), BF),
        ),
        idx,
        packed,
        packed_other,
        bmsg,
        bmsg_other,
        far_out=(0, 1),
    )
    got = [shift(msg, "x", s, NX) for s in range(1, NX)]
    ax, bx, msg = call(
        fwd_x_body,
        (
            shape((NX, 2 * n, n), BF),
            shape((NX, m, n), F32),
            shape((NZ, n + 2 * m, n // NC), BF),
        ),
        idx,
        keep,
        *got,
        *[swap(g) for g in got],
        scratch=[pltpu.VMEM((NX, 2 * n, n), BF), pltpu.VMEM((NX, m, n), F32)],
        far_out=(0, 1),
    )
    up = spread(msg, "z")

    gains, _ = lax.optimization_barrier((gains, msg))
    gfull, cpacked = call(
        bwd_local_body, (shape((steps, n, n), BF), shape((2 * n, n), BF)), idx, *gains,
        scratch=[pltpu.VMEM((steps, n, n), BF)],
        far_out=(0,),
    )
    cother = swap(cpacked)
    c32 = call(bwd_core_body, shape((2 * n, n), BF), idx, cpacked, cother)
    got = [shift(c32, "x", s, NX) for s in range(1, NX)]
    cx, cmsg = call(
        bwd_x_body,
        (shape((NX, 2 * n, n), BF), shape((NZ, n, n // NC), BF)),
        idx,
        c32,
        *got,
        scratch=[pltpu.VMEM((NX, 2 * n, n), BF)],
        far_out=(0,),
    )
    down = spread(cmsg, "z")
    b_other = call(fetch_body, shape((2 * m, n), BF), idx, far_b, far_in=(0,))
    off, fmsg = call(
        filter_body,
        (shape((steps, m, n), F32), shape((2 * m, n), BF)),
        idx,
        up,
        swap(up),
        b_other,
        far_other,
        transition,
        ax,
        bx,
        full,
        drives,
        gfull,
        scratch=[
            pltpu.VMEM((2 * n, n), BF),
            pltpu.VMEM((n, n), BF),
            pltpu.VMEM((NX, 2 * n, n), BF),
            pltpu.VMEM((NX, m, n), F32),
            pltpu.VMEM((steps, n, n), BF),
            pltpu.VMEM((steps, m, n), F32),
            pltpu.VMEM((steps, n, n), BF),
            pltpu.VMEM((steps, m, n), F32),
        ],
        far_in=(3, 4, 5, 6, 7, 8, 9),
        far_out=(0,),
    )
    fother = swap(fmsg)
    f = call(back_core_body, shape((m, n), F32), idx, fmsg, fother, cpacked, cother)
    fx, f = call(
        back_x_body,
        (shape((NX, m, n), F32), shape((NZ, m, n), F32)),
        idx,
        f,
        *[shift(f, "x", s, NX) for s in range(1, NX)],
        cx,
        scratch=[pltpu.VMEM((NX, 2 * n, n), BF)],
        far_in=(4,),
    )
    fz = spread(f, "z")
    out = call(
        smooth_body,
        (shape((half, m, 2 * w), BF),) * NR,
        idx,
        down,
        swap(down),
        fz,
        fx,
        fother,
        cother,
        cx,
        gfull,
        off,
        scratch=[
            pltpu.VMEM((NX, 2 * n, n), BF),
            pltpu.VMEM((steps, n, n), BF),
            pltpu.VMEM((steps, m, n), F32),
        ],
        far_in=(6, 7, 8),
    )
    out = out[:1] + tuple(shift(out[s], "row", s, NR) for s in range(1, NR))
    return call(
        place_body,
        shape((steps, w, members), F32),
        idx,
        *out,
        scratch=[pltpu.VMEM((NR, half, m, 2 * w), BF)],
    )


def solution(mesh):
    fine = Mesh(mesh.devices.reshape(NZ, NX, NC, NR), ("z", "x", "c", "row"))
    t = ("z", "x", "c")
    placed = (
        P(t, "row", None),
        P(t, "row", None),
        P(t, "row", None),
        P(),
        P(),
        P(t),
        P(t),
        P(t, None),
        P(t),
    )

    return jax.shard_map(
        local, mesh=fine, in_specs=placed, out_specs=P(t, "row", None), check_vma=False
    )
```

```python
import jax
import jax.numpy as jnp
from jax import lax
from jax.experimental import pallas as pl
from jax.experimental.pallas import tpu as pltpu
from jax.sharding import Mesh, PartitionSpec as P

BF = jnp.bfloat16
F32 = jnp.float32
NZ, NX, NC, NR = 8, 4, 2, 4
NQ = 4
NT = (((1,), (1,)), ((), ()))
VM = pl.BlockSpec(memory_space=pltpu.VMEM)
HB = pl.BlockSpec(memory_space=pltpu.HBM)
SM = pl.BlockSpec(memory_space=pltpu.SMEM)
AN = pl.BlockSpec(memory_space=pl.ANY)


def split(value):
    hi = value.astype(BF)
    return hi, (value - hi.astype(F32)).astype(BF)


def mm(left, right):
    return jnp.dot(left, right, preferred_element_type=F32)


def mm3(left_hi, left_lo, right_hi, right_lo):
    return mm(left_hi, right_hi) + (mm(left_hi, right_lo) + mm(left_lo, right_hi))


def push(state, weight):
    hi, lo = split(state)
    both = lax.dot_general(
        jnp.concatenate([hi, lo], axis=0), weight, NT, preferred_element_type=F32
    )
    n = state.shape[0]
    return both[:n] + both[n:]


def push2(state, weight_hi, weight_lo):
    hi, lo = split(state)
    both = lax.dot_general(
        jnp.concatenate([hi, lo], axis=0), weight_hi, NT, preferred_element_type=F32
    )
    n = state.shape[0]
    extra = lax.dot_general(hi, weight_lo, NT, preferred_element_type=F32)
    return both[:n] + (both[n:] + extra)


def coords(idx_ref):
    me = idx_ref[0]
    row = me % NR
    tm = me // NR
    return tm // (NX * NC), (tm // NC) % NX, tm % NC, row


def call(body, outs, *args, scratch=(), far_in=(), far_out=(), any_in=()):
    many = isinstance(outs, tuple)
    count = len(outs) if many else 1
    specs = tuple(HB if i in far_out else VM for i in range(count))
    far = len(far_in) + len(far_out) + len(any_in)
    if many:
        outs = tuple(
            pltpu.HBM(o.shape, o.dtype) if i in far_out else o for i, o in enumerate(outs)
        )
    args = [args[0]] + [
        pltpu.with_memory_space_constraint(a, pltpu.HBM) if i in far_in else a
        for i, a in enumerate(args[1:])
    ]
    return pl.pallas_call(
        body,
        out_shape=outs,
        in_specs=[SM]
        + [HB if i in far_in else AN if i in any_in else VM for i in range(len(args) - 1)],
        out_specs=specs if many else specs[0],
        scratch_shapes=list(scratch) + ([pltpu.SemaphoreType.DMA((far,))] if far else []),
        compiler_params=pltpu.CompilerParams(vmem_limit_bytes=16 << 20),
    )(*args)


def shape(dims, dtype):
    return jax.ShapeDtypeStruct(dims, dtype)


def drive_body(idx, basis, value, weight, time, cov, *outs):
    row = idx[0] % NR
    steps = cov.shape[0]
    weighted = (weight[...] * jnp.transpose(value[...])).astype(BF)
    local_time = time[...] - (idx[0] // NR) * steps
    half = steps // 2
    members = weighted.shape[0] // NR
    for k in range(steps):
        masked = jnp.where(local_time == k, weighted, jnp.zeros((), BF))
        info = mm(masked, basis[...]).astype(BF)
        drive = lax.dot_general(info, cov[k], NT, preferred_element_type=F32)
        w = drive.shape[1]
        lane = (k // half) * w
        for s, out in enumerate(outs):
            part = drive[0:members]
            for r in range(1, NR):
                part = jnp.where((row + s) % NR == r, drive[r * members : (r + 1) * members], part)
            out[k % half, :, lane : lane + w] = part


def assemble(row, parts, full):
    w = parts[0].shape[1]
    for s, part in enumerate(parts):
        start = pl.multiple_of(((row - s) % NR) * w, w)
        full[:, pl.ds(start, w), :] = part[...]


def tree(items, order, quads=None):
    while len(items) > 1:
        if quads is not None and len(items) == NQ:
            n = items[0][0].shape[0]
            for q, (hi, lo) in enumerate(items):
                quads[q, 0:n] = hi
                quads[q, n:] = lo
        merged = []
        for i in range(0, len(items), 2):
            left, right = order(items[i], items[i + 1])
            if left[1] is None:
                value = mm(left[0], right[0])
            else:
                value = mm3(left[0], left[1], right[0], right[1])
            merged.append(split(value))
        items = merged
    return items[0]


def later_first(a, b):
    return b, a


def earlier_first(a, b):
    return a, b


def fwd_local_body(idx, m0, m1, m2, m3, full, quads, packed):
    _, _, _, row = coords(idx)
    assemble(row, (m0, m1, m2, m3), full)
    steps, n = full.shape[0], full.shape[1]
    hi, lo = tree([(full[k], None) for k in range(steps)], later_first, quads)
    packed[0:n] = hi
    packed[n:] = lo


def fwd_drive_body(
    idx, full, quads, d0, d1, d2, d3, far_full, far_quads, far_drives, far_sums, msg,
    drv, drives, sums, sems,
):
    _, _, _, row = coords(idx)
    save_full = pltpu.make_async_copy(full, far_full, sems.at[0])
    save_full.start()
    save_quads = pltpu.make_async_copy(quads, far_quads, sems.at[2])
    save_quads.start()
    for s, part in enumerate((d0, d1, d2, d3)):
        drv[(row - s) % NR] = part[...]
    steps, n = full.shape[0], full.shape[1]
    half, w = steps // 2, n // NR
    for k in range(steps):
        lane = (k // half) * w
        drives[k] = jnp.concatenate(
            [drv[r, k % half, :, lane : lane + w] for r in range(NR)], axis=1
        )
    save_drives = pltpu.make_async_copy(drives, far_drives, sems.at[1])
    save_drives.start()
    run = steps // NQ
    chains = [drives[q * run] for q in range(NQ)]
    for j in range(1, run):
        for q in range(NQ):
            chains[q] = push(chains[q], full[q * run + j]) + drives[q * run + j]
    for q in range(NQ):
        sums[q] = chains[q]
    save_sums = pltpu.make_async_copy(sums, far_sums, sems.at[3])
    save_sums.start()
    b = chains[0]
    for q in range(1, NQ):
        b = push2(b, quads[q, 0:n], quads[q, n:]) + chains[q]
    store_pair(msg, b)
    save_full.wait()
    save_drives.wait()
    save_quads.wait()
    save_sums.wait()


def store_pair(msg, b):
    m = b.shape[0]
    hi, lo = split(b)
    msg[0:m] = hi
    msg[m:] = lo


def load_pair(msg):
    m = msg.shape[0] // 2
    return msg[0:m].astype(F32) + msg[m:].astype(F32)


def fwd_core_body(idx, own, other, b_own, b_other, far_other, far_b, keep, msg, sems):
    save_other = pltpu.make_async_copy(other, far_other, sems.at[0])
    save_b = pltpu.make_async_copy(b_other, far_b, sems.at[1])
    save_other.start()
    save_b.start()
    _, _, c, _ = coords(idx)
    n = own.shape[1]
    m = b_own.shape[0] // 2
    first = jnp.where(c == 0, own[...], other[...])
    second = jnp.where(c == 0, other[...], own[...])
    hi, lo = split(mm3(second[0:n], second[n:], first[0:n], first[n:]))
    b_mine, b_theirs = load_pair(b_own), load_pair(b_other)
    b_first = jnp.where(c == 0, b_mine, b_theirs)
    b_second = jnp.where(c == 0, b_theirs, b_mine)
    b = push2(b_first, second[0:n], second[n:]) + b_second
    w = n // NC
    keep[0:n] = hi
    keep[n : 2 * n] = lo
    b_hi, b_lo = split(b)
    keep[2 * n : 2 * n + m] = b_hi
    keep[2 * n + m :] = b_lo
    msg[0:n] = half_of(c, hi, w)
    msg[n : 2 * n] = half_of(c, lo, w)
    msg[2 * n :] = pack_vector(c, b)
    save_other.wait()
    save_b.wait()


def half_of(c, value, w):
    return jnp.where(c == 0, value[:, :w], value[:, w:])


def pack_vector(c, b):
    m, n = b.shape
    w, q = n // NC, m // NC
    hi, lo = split(jnp.where(c == 0, b[:q], b[q:]))
    return jnp.concatenate([hi[:, :w], hi[:, w:], lo[:, :w], lo[:, w:]], axis=0)


def unpack_part(msg, at, q):
    p = [msg[at + j * q : at + (j + 1) * q].astype(F32) for j in range(4)]
    return jnp.concatenate([p[0] + p[2], p[1] + p[3]], axis=1)


def unpack_vector(c, mine, other, at, m):
    q = m // NC
    a, b = unpack_part(mine, at, q), unpack_part(other, at, q)
    return jnp.concatenate([jnp.where(c == 0, a, b), jnp.where(c == 0, b, a)], axis=0)


def join(c, mine, other, rows):
    a, b = mine[0:rows], other[0:rows]
    return jnp.concatenate([jnp.where(c == 0, a, b), jnp.where(c == 0, b, a)], axis=1)


def fwd_x_body(idx, own, r1, r2, r3, s1, s2, s3, far_ax, far_bx, msg, ax, bx, sems):
    _, x, c, _ = coords(idx)
    rows, n = ax.shape[1:]
    m = bx.shape[1]
    for s, (mine, other) in enumerate(((own, None), (r1, s1), (r2, s2), (r3, s3))):
        at = (x - s) % NX
        if other is None:
            ax[at] = mine[0:rows]
            bx[at] = mine[rows : rows + m].astype(F32) + mine[rows + m :].astype(F32)
        else:
            ax[at] = join(c, mine, other, rows)
            bx[at] = unpack_vector(c, mine, other, rows, m)
    save_ax = pltpu.make_async_copy(ax, far_ax, sems.at[0])
    save_bx = pltpu.make_async_copy(bx, far_bx, sems.at[1])
    save_ax.start()
    save_bx.start()
    hi, _ = tree([(ax[i, 0:n], ax[i, n:]) for i in range(NX)], later_first)
    b = bx[0]
    for i in range(1, NX):
        b = push2(b, ax[i, 0:n], ax[i, n:]) + bx[i]
    hi = half_of(c, hi, n // NC)
    packed = pack_vector(c, b)
    for i in range(NZ):
        msg[i, 0:n] = hi
        msg[i, n:] = packed
    save_ax.wait()
    save_bx.wait()


def bwd_local_body(idx, g0, g1, g2, g3, full, quads, packed, sems):
    _, _, _, row = coords(idx)
    steps, n = full.shape[0], full.shape[1]
    w = n // NR
    copies = []
    for s, part in enumerate((g0, g1, g2, g3)):
        start = pl.multiple_of(((row - s) % NR) * w, w)
        copies.append(
            pltpu.make_async_copy(part, full.at[:, pl.ds(start, w), :], sems.at[s])
        )
        copies[-1].start()
    for copy in copies:
        copy.wait()

    @pl.when(idx[0] // NR == NZ * NX * NC - 1)
    def _():
        full[steps - 1] = jnp.zeros((n, n), BF)

    hi, lo = tree([(full[k], None) for k in range(steps)], earlier_first, quads)
    packed[0:n] = hi
    packed[n:] = lo


def bwd_core_body(idx, own, other, out, msg):
    _, _, c, _ = coords(idx)
    n = own.shape[1]
    first = jnp.where(c == 0, own[...], other[...])
    second = jnp.where(c == 0, other[...], own[...])
    hi, lo = split(mm3(first[0:n], first[n:], second[0:n], second[n:]))
    out[0:n] = hi
    out[n:] = lo
    msg[0:n] = half_of(c, hi, n // NC)
    msg[n:] = half_of(c, lo, n // NC)


def bwd_x_body(idx, own, r1, r2, r3, s1, s2, s3, far_cx, msg, cx, sems):
    _, x, c, _ = coords(idx)
    rows, n = own.shape
    cx[x] = own[...]
    for s, mine, other in ((1, r1, s1), (2, r2, s2), (3, r3, s3)):
        cx[(x - s) % NX] = join(c, mine, other, rows)
    save_cx = pltpu.make_async_copy(cx, far_cx, sems.at[0])
    save_cx.start()
    hi, _ = tree([(cx[i, 0:n], cx[i, n:]) for i in range(NX)], earlier_first)
    hi = half_of(c, hi, n // NC)
    for i in range(NZ):
        msg[i] = hi
    save_cx.wait()


def load(sems, at, *pairs):
    copies = []
    for i, (far, close) in enumerate(pairs):
        copy = pltpu.make_async_copy(far, close, sems.at[at + i])
        copy.start()
        copies.append(copy)
    return copies


def fetch_body(idx, gains, quads, far, far_gains, far_quads, out, sems):
    save_quads = pltpu.make_async_copy(quads, far_quads, sems.at[2])
    save_quads.start()
    copy = pltpu.make_async_copy(far, out, sems.at[0])
    save = pltpu.make_async_copy(gains, far_gains, sems.at[1])
    save.start()
    copy.start()
    copy.wait()
    save.wait()
    save_quads.wait()


def filter_body(
    idx, mine, swapped, b_other, far_other, far_transition, far_ax, far_bx, far_quads, far_sums,
    far_full, far_drives, far_gains, far_cquads, far_off, far_fsums, msg,
    other, transition, ax, bx, quads, sums, full, drives, gains, cquads, off, fsums, sems,
):
    z, x, c, _ = coords(idx)
    steps, n = full.shape[0], full.shape[1]
    m = drives.shape[1]
    run = steps // NQ
    (
        get_ax, get_bx, get_other, get_quads, get_sums, get_drives, get_full, get_transition,
        get_gains, get_cquads,
    ) = load(
        sems, 0, (far_ax.at[pl.ds(0, NX - 1)], ax), (far_bx, bx), (far_other, other),
        (far_quads.at[pl.ds(0, NQ - 1)], quads),
        (far_sums, sums), (far_drives, drives), (far_full, full), (far_transition, transition),
        (far_gains, gains), (far_cquads.at[pl.ds(0, NQ - 1)], cquads),
    )
    state = jnp.zeros((m, n), F32)
    for i in range(NZ - 1):
        b = unpack_vector(c, mine.at[i], swapped.at[i], n, m)
        moved = push(state, join(c, mine.at[i], swapped.at[i], n)) + b
        state = jnp.where(i < z, moved, state)
    get_ax.wait()
    get_bx.wait()
    for i in range(NX - 1):
        moved = push2(state, ax[i, 0:n], ax[i, n:]) + bx[i]
        state = jnp.where(i < x, moved, state)
    get_other.wait()
    moved = push2(state, other[0:n], other[n:]) + load_pair(b_other)
    state = jnp.where(c == 1, moved, state)
    get_quads.wait()
    get_sums.wait()
    chains = [state]
    for q in range(NQ - 1):
        chains.append(push2(chains[q], quads[q, 0:n], quads[q, n:]) + sums[q])
    get_drives.wait()
    get_full.wait()
    for j in range(run):
        for q in range(NQ):
            k = q * run + j
            chains[q] = push(chains[q], full[k]) + drives[k]
            off[k] = chains[q]
    get_transition.wait()
    weight = transition[...]
    get_gains.wait()
    moved = push(off[...].reshape(steps * m, n), weight)
    for k in range(steps):
        off[k] = off[k] - push(moved[k * m : (k + 1) * m], gains[k])
    save_off = pltpu.make_async_copy(off, far_off, sems.at[10])
    save_off.start()
    chains = [off[q * run + run - 1] for q in range(NQ)]
    for j in range(run - 2, -1, -1):
        for q in range(NQ):
            k = q * run + j
            chains[q] = push(chains[q], gains[k]) + off[k]
    for q in range(NQ):
        fsums[q] = chains[q]
    save_fsums = pltpu.make_async_copy(fsums, far_fsums, sems.at[11])
    save_fsums.start()
    get_cquads.wait()
    f = chains[NQ - 1]
    for q in range(NQ - 2, -1, -1):
        f = push2(f, cquads[q, 0:n], cquads[q, n:]) + chains[q]
    store_pair(msg, f)
    save_off.wait()
    save_fsums.wait()


def back_core_body(idx, own, other, cown, cother, out):
    _, _, c, _ = coords(idx)
    n = own.shape[1]
    f_own, f_other = load_pair(own), load_pair(other)
    f0 = jnp.where(c == 0, f_own, f_other)
    f1 = jnp.where(c == 0, f_other, f_own)
    hi = jnp.where(c == 0, cown[0:n], cother[0:n])
    lo = jnp.where(c == 0, cown[n:], cother[n:])
    out[...] = push2(f1, hi, lo) + f0


def back_x_body(idx, f0, f1, f2, f3, far_cx, fx, out, cx, sems):
    (get_cx,) = load(sems, 0, (far_cx, cx))
    _, x, _, _ = coords(idx)
    n = fx.shape[2]
    for s, part in enumerate((f0, f1, f2, f3)):
        fx[(x - s) % NX] = part[...]
    get_cx.wait()
    f = fx[NX - 1]
    for i in range(NX - 2, -1, -1):
        f = push2(f, cx[i, 0:n], cx[i, n:]) + fx[i]
    for i in range(NZ):
        out[i] = f


def smooth_body(
    idx, mine, swapped, fz, fx, fother, cother, far_cx, far_quads, far_sums, far_gains, far_off,
    o0, o1, o2, o3, cx, quads, sums, gains, off, sems,
):
    get_cx, get_quads, get_sums, get_gains, get_off = load(
        sems, 0, (far_cx, cx), (far_quads, quads), (far_sums, sums), (far_gains, gains),
        (far_off, off),
    )
    z, x, c, row = coords(idx)
    steps, n = gains.shape[0], gains.shape[1]
    m = off.shape[1]
    half, w = steps // 2, n // NR
    state = jnp.zeros((m, n), F32)
    for i in range(NZ - 1, 0, -1):
        moved = push(state, join(c, mine.at[i], swapped.at[i], n)) + fz[i].astype(F32)
        state = jnp.where(i > z, moved, state)
    get_cx.wait()
    for i in range(NX - 1, 0, -1):
        moved = push2(state, cx[i, 0:n], cx[i, n:]) + fx[i]
        state = jnp.where(i > x, moved, state)
    moved = push2(state, cother[0:n], cother[n:]) + load_pair(fother)
    state = jnp.where(c == 0, moved, state)
    get_quads.wait()
    get_sums.wait()
    chains = [state] * NQ
    for q in range(NQ - 1, 0, -1):
        chains[q - 1] = push2(chains[q], quads[q, 0:n], quads[q, n:]) + sums[q]
    get_gains.wait()
    get_off.wait()
    run = steps // NQ
    for j in range(run - 1, -1, -1):
        for q in range(NQ):
            k = q * run + j
            chains[q] = push(chains[q], gains[k]) + off[k]
            lane = (k // half) * w
            parts = [chains[q][:, r * w : (r + 1) * w].astype(BF) for r in range(NR)]
            for s, out in enumerate((o0, o1, o2, o3)):
                part = parts[0]
                for r in range(1, NR):
                    part = jnp.where((row + s) % NR == r, parts[r], part)
                out[k % half, :, lane : lane + w] = part


def place_body(idx, p0, p1, p2, p3, out, got):
    _, _, _, row = coords(idx)
    half = out.shape[0] // 2
    w = out.shape[1]
    for s, part in enumerate((p0, p1, p2, p3)):
        got[(row - s) % NR] = part[...]
    for k in range(half):
        block = jnp.concatenate([got[r, k] for r in range(NR)], axis=0).astype(F32)
        turned = jnp.transpose(block)
        out[k] = turned[:w]
        out[k + half] = turned[w:]


def shift(value, axis, step, size):
    return lax.ppermute(value, axis, [(i, (i + step) % size) for i in range(size)])


def spread(value, axis):
    return lax.all_to_all(value, axis, 0, 0, tiled=True)


def swap(value):
    return lax.ppermute(value, "c", [(0, 1), (1, 0)])


def gather_rows(value):
    return [value] + [shift(value, "row", s, NR) for s in range(1, NR)]


def local(
    filter_map,
    filter_cov,
    smoother_gain,
    transition,
    site_basis,
    obs_time,
    obs_site,
    obs_value,
    obs_weight,
):
    steps, w, n = filter_map.shape
    obs, members = obs_value.shape
    m = members // NR
    half = steps // 2
    tm = (lax.axis_index("z") * NX + lax.axis_index("x")) * NC + lax.axis_index("c")
    idx = (tm * NR + lax.axis_index("row")).astype(jnp.int32).reshape(1)

    maps = gather_rows(filter_map)
    basis_rows = site_basis.at[obs_site].get(mode="promise_in_bounds")
    drive = call(
        drive_body,
        (shape((half, m, 2 * w), F32),) * NR,
        idx,
        basis_rows,
        obs_value,
        obs_weight.reshape(1, obs),
        obs_time.reshape(1, obs),
        filter_cov,
    )
    gain_in, _ = lax.optimization_barrier((smoother_gain, drive))
    drive = drive[:1] + tuple(shift(drive[s], "row", s, NR) for s in range(1, NR))
    gains = gather_rows(gain_in)
    full, quads, packed = call(
        fwd_local_body,
        (shape((steps, n, n), BF), shape((NQ, 2 * n, n), BF), shape((2 * n, n), BF)),
        idx,
        *maps,
    )
    packed_other = swap(packed)
    full, quads, drives, sums, bmsg = call(
        fwd_drive_body,
        (
            shape((steps, n, n), BF),
            shape((NQ, 2 * n, n), BF),
            shape((steps, m, n), F32),
            shape((NQ, m, n), F32),
            shape((2 * m, n), BF),
        ),
        idx,
        full,
        quads,
        *drive,
        scratch=[
            pltpu.VMEM((NR, half, m, 2 * w), F32),
            pltpu.VMEM((steps, m, n), F32),
            pltpu.VMEM((NQ, m, n), F32),
        ],
        far_out=(0, 1, 2, 3),
    )
    bmsg_other = swap(bmsg)
    far_other, far_b, keep, msg = call(
        fwd_core_body,
        (
            shape((2 * n, n), BF),
            shape((2 * m, n), BF),
            shape((2 * n + 2 * m, n), BF),
            shape((2 * n + 2 * m, n // NC), BF),
        ),
        idx,
        packed,
        packed_other,
        bmsg,
        bmsg_other,
        far_out=(0, 1),
    )
    got = [shift(msg, "x", s, NX) for s in range(1, NX)]
    ax, bx, msg = call(
        fwd_x_body,
        (
            shape((NX, 2 * n, n), BF),
            shape((NX, m, n), F32),
            shape((NZ, n + 2 * m, n // NC), BF),
        ),
        idx,
        keep,
        *got,
        *[swap(g) for g in got],
        scratch=[pltpu.VMEM((NX, 2 * n, n), BF), pltpu.VMEM((NX, m, n), F32)],
        far_out=(0, 1),
    )
    up = spread(msg, "z")

    gains, _ = lax.optimization_barrier((gains, msg))
    gfull, cquads, cpacked = call(
        bwd_local_body,
        (shape((steps, n, n), BF), shape((NQ, 2 * n, n), BF), shape((2 * n, n), BF)),
        idx,
        *gains,
        any_in=(0, 1, 2, 3),
    )
    cother = swap(cpacked)
    c32, cmsg = call(
        bwd_core_body,
        (shape((2 * n, n), BF), shape((2 * n, n // NC), BF)),
        idx,
        cpacked,
        cother,
    )
    got = [shift(cmsg, "x", s, NX) for s in range(1, NX)]
    cx, cmsg = call(
        bwd_x_body,
        (shape((NX, 2 * n, n), BF), shape((NZ, n, n // NC), BF)),
        idx,
        c32,
        *got,
        *[swap(g) for g in got],
        scratch=[pltpu.VMEM((NX, 2 * n, n), BF)],
        far_out=(0,),
    )
    down = spread(cmsg, "z")
    gfull, cquads, b_other = call(
        fetch_body,
        (shape((steps, n, n), BF), shape((NQ, 2 * n, n), BF), shape((2 * m, n), BF)),
        idx,
        gfull,
        cquads,
        far_b,
        far_in=(2,),
        far_out=(0, 1),
    )
    up_other = swap(up)
    off, fsums, fmsg = call(
        filter_body,
        (shape((steps, m, n), F32), shape((NQ, m, n), F32), shape((2 * m, n), BF)),
        idx,
        up,
        up_other,
        b_other,
        far_other,
        transition,
        ax,
        bx,
        quads,
        sums,
        full,
        drives,
        gfull,
        cquads,
        scratch=[
            pltpu.VMEM((2 * n, n), BF),
            pltpu.VMEM((n, n), BF),
            pltpu.VMEM((NX - 1, 2 * n, n), BF),
            pltpu.VMEM((NX, m, n), F32),
            pltpu.VMEM((NQ - 1, 2 * n, n), BF),
            pltpu.VMEM((NQ, m, n), F32),
            pltpu.VMEM((steps, n, n), BF),
            pltpu.VMEM((steps, m, n), F32),
            pltpu.VMEM((steps, n, n), BF),
            pltpu.VMEM((NQ - 1, 2 * n, n), BF),
            pltpu.VMEM((steps, m, n), F32),
            pltpu.VMEM((NQ, m, n), F32),
        ],
        far_in=(3, 4, 5, 6, 7, 8, 9, 10, 11, 12),
        far_out=(0, 1),
    )
    fother = swap(fmsg)
    f = call(back_core_body, shape((m, n), F32), idx, fmsg, fother, cpacked, cother)
    fx, f = call(
        back_x_body,
        (shape((NX, m, n), F32), shape((NZ, m, n), F32)),
        idx,
        f,
        *[shift(f, "x", s, NX) for s in range(1, NX)],
        cx,
        scratch=[pltpu.VMEM((NX, 2 * n, n), BF)],
        far_in=(4,),
    )
    fz = spread(f, "z")
    out = call(
        smooth_body,
        (shape((half, m, 2 * w), BF),) * NR,
        idx,
        down,
        swap(down),
        fz,
        fx,
        fother,
        cother,
        cx,
        cquads,
        fsums,
        gfull,
        off,
        scratch=[
            pltpu.VMEM((NX, 2 * n, n), BF),
            pltpu.VMEM((NQ, 2 * n, n), BF),
            pltpu.VMEM((NQ, m, n), F32),
            pltpu.VMEM((steps, n, n), BF),
            pltpu.VMEM((steps, m, n), F32),
        ],
        far_in=(6, 7, 8, 9, 10),
    )
    out = out[:1] + tuple(shift(out[s], "row", s, NR) for s in range(1, NR))
    return call(
        place_body,
        shape((steps, w, members), F32),
        idx,
        *out,
        scratch=[pltpu.VMEM((NR, half, m, 2 * w), BF)],
    )


def solution(mesh):
    fine = Mesh(mesh.devices.reshape(NZ, NX, NC, NR), ("z", "x", "c", "row"))
    t = ("z", "x", "c")
    placed = (
        P(t, "row", None),
        P(t, "row", None),
        P(t, "row", None),
        P(),
        P(),
        P(t),
        P(t),
        P(t, None),
        P(t),
    )

    return jax.shard_map(
        local, mesh=fine, in_specs=placed, out_specs=P(t, "row", None), check_vma=False
    )
```

```python
import jax
import jax.numpy as jnp
from jax import lax
from jax.experimental import pallas as pl
from jax.experimental.pallas import tpu as pltpu
from jax.sharding import Mesh, PartitionSpec as P

BF = jnp.bfloat16
F32 = jnp.float32
NZ, NX, NC, NR = 8, 4, 2, 4
NQ = 4
NT = (((1,), (1,)), ((), ()))
VM = pl.BlockSpec(memory_space=pltpu.VMEM)
HB = pl.BlockSpec(memory_space=pltpu.HBM)
SM = pl.BlockSpec(memory_space=pltpu.SMEM)
AN = pl.BlockSpec(memory_space=pl.ANY)


def split(value):
    hi = value.astype(BF)
    return hi, (value - hi.astype(F32)).astype(BF)


def mm(left, right):
    return jnp.dot(left, right, preferred_element_type=F32)


def mm3(left_hi, left_lo, right_hi, right_lo):
    return mm(left_hi, right_hi) + (mm(left_hi, right_lo) + mm(left_lo, right_hi))


def push(state, weight):
    hi, lo = split(state)
    both = lax.dot_general(
        jnp.concatenate([hi, lo], axis=0), weight, NT, preferred_element_type=F32
    )
    n = state.shape[0]
    return both[:n] + both[n:]


def push2(state, weight_hi, weight_lo):
    hi, lo = split(state)
    both = lax.dot_general(
        jnp.concatenate([hi, lo], axis=0), weight_hi, NT, preferred_element_type=F32
    )
    n = state.shape[0]
    extra = lax.dot_general(hi, weight_lo, NT, preferred_element_type=F32)
    return both[:n] + (both[n:] + extra)


def coords(idx_ref):
    me = idx_ref[0]
    row = me % NR
    tm = me // NR
    return tm // (NX * NC), (tm // NC) % NX, tm % NC, row


def call(body, outs, *args, scratch=(), far_in=(), far_out=(), any_in=()):
    many = isinstance(outs, tuple)
    count = len(outs) if many else 1
    specs = tuple(HB if i in far_out else VM for i in range(count))
    far = len(far_in) + len(far_out) + len(any_in)
    if many:
        outs = tuple(
            pltpu.HBM(o.shape, o.dtype) if i in far_out else o for i, o in enumerate(outs)
        )
    args = [args[0]] + [
        pltpu.with_memory_space_constraint(a, pltpu.HBM) if i in far_in else a
        for i, a in enumerate(args[1:])
    ]
    return pl.pallas_call(
        body,
        out_shape=outs,
        in_specs=[SM]
        + [HB if i in far_in else AN if i in any_in else VM for i in range(len(args) - 1)],
        out_specs=specs if many else specs[0],
        scratch_shapes=list(scratch) + ([pltpu.SemaphoreType.DMA((far,))] if far else []),
        compiler_params=pltpu.CompilerParams(vmem_limit_bytes=16 << 20),
    )(*args)


def shape(dims, dtype):
    return jax.ShapeDtypeStruct(dims, dtype)


def drive_body(idx, basis, value, weight, time, cov, *outs):
    row = idx[0] % NR
    steps = cov.shape[0]
    weighted = (weight[...] * jnp.transpose(value[...])).astype(BF)
    local_time = time[...] - (idx[0] // NR) * steps
    half = steps // 2
    members = weighted.shape[0] // NR
    for k in range(steps):
        masked = jnp.where(local_time == k, weighted, jnp.zeros((), BF))
        info = mm(masked, basis[...]).astype(BF)
        drive = lax.dot_general(info, cov[k], NT, preferred_element_type=F32)
        w = drive.shape[1]
        lane = (k // half) * w
        for s, out in enumerate(outs):
            part = drive[0:members]
            for r in range(1, NR):
                part = jnp.where((row + s) % NR == r, drive[r * members : (r + 1) * members], part)
            out[k % half, :, lane : lane + w] = part


def assemble(row, parts, full):
    w = parts[0].shape[1]
    for s, part in enumerate(parts):
        start = pl.multiple_of(((row - s) % NR) * w, w)
        full[:, pl.ds(start, w), :] = part[...]


def tree(items, order, quads=None):
    while len(items) > 1:
        if quads is not None and len(items) == NQ:
            n = items[0][0].shape[0]
            for q, (hi, lo) in enumerate(items):
                quads[q, 0:n] = hi
                quads[q, n:] = lo
        merged = []
        for i in range(0, len(items), 2):
            left, right = order(items[i], items[i + 1])
            if left[1] is None:
                value = mm(left[0], right[0])
            else:
                value = mm3(left[0], left[1], right[0], right[1])
            merged.append(split(value))
        items = merged
    return items[0]


def later_first(a, b):
    return b, a


def earlier_first(a, b):
    return a, b


def fwd_local_body(idx, m0, m1, m2, m3, full, quads, packed):
    _, _, _, row = coords(idx)
    assemble(row, (m0, m1, m2, m3), full)
    steps, n = full.shape[0], full.shape[1]
    hi, lo = tree([(full[k], None) for k in range(steps)], later_first, quads)
    packed[0:n] = hi
    packed[n:] = lo


def fwd_drive_body(
    idx, full, quads, d0, d1, d2, d3, far_full, far_quads, far_drives, far_sums, msg,
    drv, drives, sums, sems,
):
    _, _, _, row = coords(idx)
    save_full = pltpu.make_async_copy(full, far_full, sems.at[0])
    save_full.start()
    save_quads = pltpu.make_async_copy(quads, far_quads, sems.at[2])
    save_quads.start()
    for s, part in enumerate((d0, d1, d2, d3)):
        drv[(row - s) % NR] = part[...]
    steps, n = full.shape[0], full.shape[1]
    half, w = steps // 2, n // NR
    for k in range(steps):
        lane = (k // half) * w
        drives[k] = jnp.concatenate(
            [drv[r, k % half, :, lane : lane + w] for r in range(NR)], axis=1
        )
    save_drives = pltpu.make_async_copy(drives, far_drives, sems.at[1])
    save_drives.start()
    run = steps // NQ
    chains = [drives[q * run] for q in range(NQ)]
    for j in range(1, run):
        for q in range(NQ):
            chains[q] = push(chains[q], full[q * run + j]) + drives[q * run + j]
    for q in range(NQ):
        sums[q] = chains[q]
    save_sums = pltpu.make_async_copy(sums, far_sums, sems.at[3])
    save_sums.start()
    b = chains[0]
    for q in range(1, NQ):
        b = push2(b, quads[q, 0:n], quads[q, n:]) + chains[q]
    store_pair(msg, b)
    save_full.wait()
    save_drives.wait()
    save_quads.wait()
    save_sums.wait()


def store_pair(msg, b):
    m = b.shape[0]
    hi, lo = split(b)
    msg[0:m] = hi
    msg[m:] = lo


def load_pair(msg):
    m = msg.shape[0] // 2
    return msg[0:m].astype(F32) + msg[m:].astype(F32)


def fwd_core_body(idx, own, other, b_own, b_other, far_other, far_b, keep, msg, sems):
    save_other = pltpu.make_async_copy(other, far_other, sems.at[0])
    save_b = pltpu.make_async_copy(b_other, far_b, sems.at[1])
    save_other.start()
    save_b.start()
    _, _, c, _ = coords(idx)
    n = own.shape[1]
    m = b_own.shape[0] // 2
    first = jnp.where(c == 0, own[...], other[...])
    second = jnp.where(c == 0, other[...], own[...])
    hi, lo = split(mm3(second[0:n], second[n:], first[0:n], first[n:]))
    b_mine, b_theirs = load_pair(b_own), load_pair(b_other)
    b_first = jnp.where(c == 0, b_mine, b_theirs)
    b_second = jnp.where(c == 0, b_theirs, b_mine)
    b = push2(b_first, second[0:n], second[n:]) + b_second
    w = n // NC
    keep[0:n] = hi
    keep[n : 2 * n] = lo
    b_hi, b_lo = split(b)
    keep[2 * n : 2 * n + m] = b_hi
    keep[2 * n + m :] = b_lo
    msg[0:n] = half_of(c, hi, w)
    msg[n : 2 * n] = half_of(c, lo, w)
    msg[2 * n :] = pack_vector(c, b)
    save_other.wait()
    save_b.wait()


def half_of(c, value, w):
    return jnp.where(c == 0, value[:, :w], value[:, w:])


def pack_vector(c, b):
    m, n = b.shape
    w, q = n // NC, m // NC
    hi, lo = split(jnp.where(c == 0, b[:q], b[q:]))
    return jnp.concatenate([hi[:, :w], hi[:, w:], lo[:, :w], lo[:, w:]], axis=0)


def unpack_part(msg, at, q):
    p = [msg[at + j * q : at + (j + 1) * q].astype(F32) for j in range(4)]
    return jnp.concatenate([p[0] + p[2], p[1] + p[3]], axis=1)


def unpack_vector(c, mine, other, at, m):
    q = m // NC
    a, b = unpack_part(mine, at, q), unpack_part(other, at, q)
    return jnp.concatenate([jnp.where(c == 0, a, b), jnp.where(c == 0, b, a)], axis=0)


def join(c, mine, other, rows):
    a, b = mine[0:rows], other[0:rows]
    return jnp.concatenate([jnp.where(c == 0, a, b), jnp.where(c == 0, b, a)], axis=1)


def fwd_x_body(idx, own, r1, r2, r3, s1, s2, s3, far_ax, far_bx, msg, ax, bx, sems):
    _, x, c, _ = coords(idx)
    rows, n = ax.shape[1:]
    m = bx.shape[1]
    for s, (mine, other) in enumerate(((own, None), (r1, s1), (r2, s2), (r3, s3))):
        at = (x - s) % NX
        if other is None:
            ax[at] = mine[0:rows]
            bx[at] = mine[rows : rows + m].astype(F32) + mine[rows + m :].astype(F32)
        else:
            ax[at] = join(c, mine, other, rows)
            bx[at] = unpack_vector(c, mine, other, rows, m)
    save_ax = pltpu.make_async_copy(ax, far_ax, sems.at[0])
    save_bx = pltpu.make_async_copy(bx, far_bx, sems.at[1])
    save_ax.start()
    save_bx.start()
    hi, _ = tree([(ax[i, 0:n], ax[i, n:]) for i in range(NX)], later_first)
    b = bx[0]
    for i in range(1, NX):
        b = push2(b, ax[i, 0:n], ax[i, n:]) + bx[i]
    hi = half_of(c, hi, n // NC)
    packed = pack_vector(c, b)
    for i in range(NZ):
        msg[i, 0:n] = hi
        msg[i, n:] = packed
    save_ax.wait()
    save_bx.wait()


def bwd_local_body(idx, g0, g1, g2, g3, full, quads, packed, sems):
    _, _, _, row = coords(idx)
    steps, n = full.shape[0], full.shape[1]
    w = n // NR
    copies = []
    for s, part in enumerate((g0, g1, g2, g3)):
        start = pl.multiple_of(((row - s) % NR) * w, w)
        copies.append(
            pltpu.make_async_copy(part, full.at[:, pl.ds(start, w), :], sems.at[s])
        )
        copies[-1].start()
    for copy in copies:
        copy.wait()

    @pl.when(idx[0] // NR == NZ * NX * NC - 1)
    def _():
        full[steps - 1] = jnp.zeros((n, n), BF)

    hi, lo = tree([(full[k], None) for k in range(steps)], earlier_first, quads)
    packed[0:n] = hi
    packed[n:] = lo


def bwd_core_body(idx, own, other, out, msg):
    _, _, c, _ = coords(idx)
    n = own.shape[1]
    first = jnp.where(c == 0, own[...], other[...])
    second = jnp.where(c == 0, other[...], own[...])
    hi, lo = split(mm3(first[0:n], first[n:], second[0:n], second[n:]))
    out[0:n] = hi
    out[n:] = lo
    msg[0:n] = half_of(c, hi, n // NC)
    msg[n:] = half_of(c, lo, n // NC)


def bwd_x_body(idx, own, r1, r2, r3, s1, s2, s3, far_cx, msg, cx, sems):
    _, x, c, _ = coords(idx)
    rows, n = own.shape
    cx[x] = own[...]
    for s, mine, other in ((1, r1, s1), (2, r2, s2), (3, r3, s3)):
        cx[(x - s) % NX] = join(c, mine, other, rows)
    save_cx = pltpu.make_async_copy(cx, far_cx, sems.at[0])
    save_cx.start()
    hi, _ = tree([(cx[i, 0:n], cx[i, n:]) for i in range(NX)], earlier_first)
    hi = half_of(c, hi, n // NC)
    for i in range(NZ):
        msg[i] = hi
    save_cx.wait()


def load(sems, at, *pairs):
    copies = []
    for i, (far, close) in enumerate(pairs):
        copy = pltpu.make_async_copy(far, close, sems.at[at + i])
        copy.start()
        copies.append(copy)
    return copies


def fetch_body(idx, gains, quads, far, far_gains, far_quads, out, sems):
    save_quads = pltpu.make_async_copy(quads, far_quads, sems.at[2])
    save_quads.start()
    copy = pltpu.make_async_copy(far, out, sems.at[0])
    save = pltpu.make_async_copy(gains, far_gains, sems.at[1])
    save.start()
    copy.start()
    copy.wait()
    save.wait()
    save_quads.wait()


def filter_body(
    idx, mine, swapped, b_other, far_other, far_transition, far_ax, far_bx, far_quads, far_sums,
    far_full, far_drives, far_gains, far_cquads, far_off, far_fsums, msg,
    other, transition, ax, bx, quads, sums, full, drives, gains, cquads, off, fsums, sems,
):
    z, x, c, _ = coords(idx)
    steps, n = full.shape[0], full.shape[1]
    m = drives.shape[1]
    run = steps // NQ
    (
        get_ax, get_bx, get_other, get_quads, get_sums, get_drives, get_full, get_transition,
        get_gains, get_cquads,
    ) = load(
        sems, 0, (far_ax.at[pl.ds(0, NX - 1)], ax), (far_bx, bx), (far_other, other),
        (far_quads.at[pl.ds(0, NQ - 1)], quads),
        (far_sums, sums), (far_drives, drives), (far_full, full), (far_transition, transition),
        (far_gains, gains), (far_cquads.at[pl.ds(0, NQ - 1)], cquads),
    )
    state = jnp.zeros((m, n), F32)
    for i in range(NZ - 1):
        b = unpack_vector(c, mine.at[i], swapped.at[i], n, m)
        moved = push(state, join(c, mine.at[i], swapped.at[i], n)) + b
        state = jnp.where(i < z, moved, state)
    get_ax.wait()
    get_bx.wait()
    for i in range(NX - 1):
        moved = push2(state, ax[i, 0:n], ax[i, n:]) + bx[i]
        state = jnp.where(i < x, moved, state)
    get_other.wait()
    moved = push2(state, other[0:n], other[n:]) + load_pair(b_other)
    state = jnp.where(c == 1, moved, state)
    get_quads.wait()
    get_sums.wait()
    chains = [state]
    for q in range(NQ - 1):
        chains.append(push2(chains[q], quads[q, 0:n], quads[q, n:]) + sums[q])
    get_drives.wait()
    get_full.wait()
    for j in range(run):
        for q in range(NQ):
            k = q * run + j
            chains[q] = push(chains[q], full[k]) + drives[k]
            off[k] = chains[q]
    get_transition.wait()
    weight = transition[...]
    get_gains.wait()
    moved = push(off[...].reshape(steps * m, n), weight)
    for k in range(steps):
        off[k] = off[k] - push(moved[k * m : (k + 1) * m], gains[k])
    save_off = pltpu.make_async_copy(off, far_off, sems.at[10])
    save_off.start()
    chains = [off[q * run + run - 1] for q in range(NQ)]
    for j in range(run - 2, -1, -1):
        for q in range(NQ):
            k = q * run + j
            chains[q] = push(chains[q], gains[k]) + off[k]
    for q in range(NQ):
        fsums[q] = chains[q]
    save_fsums = pltpu.make_async_copy(fsums, far_fsums, sems.at[11])
    save_fsums.start()
    get_cquads.wait()
    f = chains[NQ - 1]
    for q in range(NQ - 2, -1, -1):
        f = push2(f, cquads[q, 0:n], cquads[q, n:]) + chains[q]
    store_pair(msg, f)
    save_off.wait()
    save_fsums.wait()


def back_core_body(idx, own, other, cown, cother, out):
    _, _, c, _ = coords(idx)
    n = own.shape[1]
    f_own, f_other = load_pair(own), load_pair(other)
    f0 = jnp.where(c == 0, f_own, f_other)
    f1 = jnp.where(c == 0, f_other, f_own)
    hi = jnp.where(c == 0, cown[0:n], cother[0:n])
    lo = jnp.where(c == 0, cown[n:], cother[n:])
    out[...] = push2(f1, hi, lo) + f0


def back_x_body(idx, f0, f1, f2, f3, far_cx, fx, out, cx, sems):
    (get_cx,) = load(sems, 0, (far_cx, cx))
    _, x, _, _ = coords(idx)
    n = fx.shape[2]
    for s, part in enumerate((f0, f1, f2, f3)):
        fx[(x - s) % NX] = part[...]
    get_cx.wait()
    f = fx[NX - 1]
    for i in range(NX - 2, -1, -1):
        f = push2(f, cx[i, 0:n], cx[i, n:]) + fx[i]
    for i in range(NZ):
        out[i] = f


def smooth_body(
    idx, mine, swapped, fz, fx, fother, cother, far_cx, far_quads, far_sums, far_gains, far_off,
    o0, o1, o2, o3, cx, quads, sums, gains, off, sems,
):
    get_cx, get_quads, get_sums, get_gains, get_off = load(
        sems, 0, (far_cx, cx), (far_quads, quads), (far_sums, sums), (far_gains, gains),
        (far_off, off),
    )
    z, x, c, row = coords(idx)
    steps, n = gains.shape[0], gains.shape[1]
    m = off.shape[1]
    half, w = steps // 2, n // NR
    state = jnp.zeros((m, n), F32)
    for i in range(NZ - 1, 0, -1):
        moved = push(state, join(c, mine.at[i], swapped.at[i], n)) + fz[i].astype(F32)
        state = jnp.where(i > z, moved, state)
    get_cx.wait()
    for i in range(NX - 1, 0, -1):
        moved = push2(state, cx[i, 0:n], cx[i, n:]) + fx[i]
        state = jnp.where(i > x, moved, state)
    moved = push2(state, cother[0:n], cother[n:]) + load_pair(fother)
    state = jnp.where(c == 0, moved, state)
    get_quads.wait()
    get_sums.wait()
    chains = [state] * NQ
    for q in range(NQ - 1, 0, -1):
        chains[q - 1] = push2(chains[q], quads[q, 0:n], quads[q, n:]) + sums[q]
    get_gains.wait()
    get_off.wait()
    run = steps // NQ
    for j in range(run - 1, -1, -1):
        for q in range(NQ):
            k = q * run + j
            chains[q] = push(chains[q], gains[k]) + off[k]
            lane = (k // half) * w
            parts = [chains[q][:, r * w : (r + 1) * w] for r in range(NR)]
            for s, out in enumerate((o0, o1, o2, o3)):
                part = parts[0]
                for r in range(1, NR):
                    part = jnp.where((row + s) % NR == r, parts[r], part)
                out[k % half, :, lane : lane + w] = part


def place_body(idx, p0, p1, p2, p3, out, got):
    _, _, _, row = coords(idx)
    half = out.shape[0] // 2
    w = out.shape[1]
    for s, part in enumerate((p0, p1, p2, p3)):
        got[(row - s) % NR] = part[...]
    for k in range(half):
        block = jnp.concatenate([got[r, k] for r in range(NR)], axis=0)
        turned = jnp.transpose(block)
        out[k] = turned[:w]
        out[k + half] = turned[w:]


def shift(value, axis, step, size):
    return lax.ppermute(value, axis, [(i, (i + step) % size) for i in range(size)])


def spread(value, axis):
    return lax.all_to_all(value, axis, 0, 0, tiled=True)


def swap(value):
    return lax.ppermute(value, "c", [(0, 1), (1, 0)])


def gather_rows(value):
    return [value] + [shift(value, "row", s, NR) for s in range(1, NR)]


def local(
    filter_map,
    filter_cov,
    smoother_gain,
    transition,
    site_basis,
    obs_time,
    obs_site,
    obs_value,
    obs_weight,
):
    steps, w, n = filter_map.shape
    obs, members = obs_value.shape
    m = members // NR
    half = steps // 2
    tm = (lax.axis_index("z") * NX + lax.axis_index("x")) * NC + lax.axis_index("c")
    idx = (tm * NR + lax.axis_index("row")).astype(jnp.int32).reshape(1)

    maps = gather_rows(filter_map)
    basis_rows = site_basis.at[obs_site].get(mode="promise_in_bounds")
    drive = call(
        drive_body,
        (shape((half, m, 2 * w), F32),) * NR,
        idx,
        basis_rows,
        obs_value,
        obs_weight.reshape(1, obs),
        obs_time.reshape(1, obs),
        filter_cov,
    )
    gain_in, _ = lax.optimization_barrier((smoother_gain, drive))
    drive = drive[:1] + tuple(shift(drive[s], "row", s, NR) for s in range(1, NR))
    gains = gather_rows(gain_in)
    full, quads, packed = call(
        fwd_local_body,
        (shape((steps, n, n), BF), shape((NQ, 2 * n, n), BF), shape((2 * n, n), BF)),
        idx,
        *maps,
    )
    packed_other = swap(packed)
    full, quads, drives, sums, bmsg = call(
        fwd_drive_body,
        (
            shape((steps, n, n), BF),
            shape((NQ, 2 * n, n), BF),
            shape((steps, m, n), F32),
            shape((NQ, m, n), F32),
            shape((2 * m, n), BF),
        ),
        idx,
        full,
        quads,
        *drive,
        scratch=[
            pltpu.VMEM((NR, half, m, 2 * w), F32),
            pltpu.VMEM((steps, m, n), F32),
            pltpu.VMEM((NQ, m, n), F32),
        ],
        far_out=(0, 1, 2, 3),
    )
    bmsg_other = swap(bmsg)
    far_other, far_b, keep, msg = call(
        fwd_core_body,
        (
            shape((2 * n, n), BF),
            shape((2 * m, n), BF),
            shape((2 * n + 2 * m, n), BF),
            shape((2 * n + 2 * m, n // NC), BF),
        ),
        idx,
        packed,
        packed_other,
        bmsg,
        bmsg_other,
        far_out=(0, 1),
    )
    got = [shift(msg, "x", s, NX) for s in range(1, NX)]
    ax, bx, msg = call(
        fwd_x_body,
        (
            shape((NX, 2 * n, n), BF),
            shape((NX, m, n), F32),
            shape((NZ, n + 2 * m, n // NC), BF),
        ),
        idx,
        keep,
        *got,
        *[swap(g) for g in got],
        scratch=[pltpu.VMEM((NX, 2 * n, n), BF), pltpu.VMEM((NX, m, n), F32)],
        far_out=(0, 1),
    )
    up = spread(msg, "z")

    gains, _ = lax.optimization_barrier((gains, msg))
    gfull, cquads, cpacked = call(
        bwd_local_body,
        (shape((steps, n, n), BF), shape((NQ, 2 * n, n), BF), shape((2 * n, n), BF)),
        idx,
        *gains,
        any_in=(0, 1, 2, 3),
    )
    cother = swap(cpacked)
    c32, cmsg = call(
        bwd_core_body,
        (shape((2 * n, n), BF), shape((2 * n, n // NC), BF)),
        idx,
        cpacked,
        cother,
    )
    got = [shift(cmsg, "x", s, NX) for s in range(1, NX)]
    cx, cmsg = call(
        bwd_x_body,
        (shape((NX, 2 * n, n), BF), shape((NZ, n, n // NC), BF)),
        idx,
        c32,
        *got,
        *[swap(g) for g in got],
        scratch=[pltpu.VMEM((NX, 2 * n, n), BF)],
        far_out=(0,),
    )
    down = spread(cmsg, "z")
    gfull, cquads, b_other = call(
        fetch_body,
        (shape((steps, n, n), BF), shape((NQ, 2 * n, n), BF), shape((2 * m, n), BF)),
        idx,
        gfull,
        cquads,
        far_b,
        far_in=(2,),
        far_out=(0, 1),
    )
    up_other = swap(up)
    off, fsums, fmsg = call(
        filter_body,
        (shape((steps, m, n), F32), shape((NQ, m, n), F32), shape((2 * m, n), BF)),
        idx,
        up,
        up_other,
        b_other,
        far_other,
        transition,
        ax,
        bx,
        quads,
        sums,
        full,
        drives,
        gfull,
        cquads,
        scratch=[
            pltpu.VMEM((2 * n, n), BF),
            pltpu.VMEM((n, n), BF),
            pltpu.VMEM((NX - 1, 2 * n, n), BF),
            pltpu.VMEM((NX, m, n), F32),
            pltpu.VMEM((NQ - 1, 2 * n, n), BF),
            pltpu.VMEM((NQ, m, n), F32),
            pltpu.VMEM((steps, n, n), BF),
            pltpu.VMEM((steps, m, n), F32),
            pltpu.VMEM((steps, n, n), BF),
            pltpu.VMEM((NQ - 1, 2 * n, n), BF),
            pltpu.VMEM((steps, m, n), F32),
            pltpu.VMEM((NQ, m, n), F32),
        ],
        far_in=(3, 4, 5, 6, 7, 8, 9, 10, 11, 12),
        far_out=(0, 1),
    )
    fother = swap(fmsg)
    f = call(back_core_body, shape((m, n), F32), idx, fmsg, fother, cpacked, cother)
    fx, f = call(
        back_x_body,
        (shape((NX, m, n), F32), shape((NZ, m, n), F32)),
        idx,
        f,
        *[shift(f, "x", s, NX) for s in range(1, NX)],
        cx,
        scratch=[pltpu.VMEM((NX, 2 * n, n), BF)],
        far_in=(4,),
    )
    fz = spread(f, "z")
    out = call(
        smooth_body,
        (shape((half, m, 2 * w), F32),) * NR,
        idx,
        down,
        swap(down),
        fz,
        fx,
        fother,
        cother,
        cx,
        cquads,
        fsums,
        gfull,
        off,
        scratch=[
            pltpu.VMEM((NX, 2 * n, n), BF),
            pltpu.VMEM((NQ, 2 * n, n), BF),
            pltpu.VMEM((NQ, m, n), F32),
            pltpu.VMEM((steps, n, n), BF),
            pltpu.VMEM((steps, m, n), F32),
        ],
        far_in=(6, 7, 8, 9, 10),
    )
    out = out[:1] + tuple(shift(out[s], "row", s, NR) for s in range(1, NR))
    return call(
        place_body,
        shape((steps, w, members), F32),
        idx,
        *out,
        scratch=[pltpu.VMEM((NR, half, m, 2 * w), F32)],
    )


def solution(mesh):
    fine = Mesh(mesh.devices.reshape(NZ, NX, NC, NR), ("z", "x", "c", "row"))
    t = ("z", "x", "c")
    placed = (
        P(t, "row", None),
        P(t, "row", None),
        P(t, "row", None),
        P(),
        P(),
        P(t),
        P(t),
        P(t, None),
        P(t),
    )

    return jax.shard_map(
        local, mesh=fine, in_specs=placed, out_specs=P(t, "row", None), check_vma=False
    )
```
